32 devices in a mesh: gx: 4 (over z), gy: 4 (over y, core), gz: 2 (over x).
Axes of the slice: x: 2, y: 2, z: 4, core: 2. Of those that a mesh axis runs over, the one named last changes fastest.
Arguments:
- velocities: float32 [3, 1310720], P(None, ('gx', 'gy', 'gz')), may hold values from -6 to 6
- particle_cells: int32 [2, 1310720], P(None, ('gx', 'gy', 'gz')), may hold values from 0 to 4095
- grid_shift: int32 [2, 3], replicated, may hold values from -1 to 1, as said below
- axis_index: int32 [2, 16, 32, 256], P(None, 'gx', 'gy', 'gz'), may hold values from 0 to 7
- migrate_dir: int32 [1310720], P(('gx', 'gy', 'gz')), may hold values from 0 to 6, as said below
- migrate_slot: int32 [1310720], P(('gx', 'gy', 'gz')), may hold values from 0 to 159, as said below
- contact_colloid: int32 [65536], P(('gx', 'gy', 'gz')), may hold values from 0 to 8191, as said below
- contact_particle: int32 [65536], P(('gx', 'gy', 'gz')), may hold values from 0 to 40959
- contact_weight: float32 [65536], P(('gx', 'gy', 'gz')), may hold values from 0.05 to 1
- colloid_velocity: float32 [3, 8192], P(None, ('gx', 'gy', 'gz')), may hold values from -6 to 6
Outputs:
- cell_velocity: float32 [3, 16, 32, 256], P(None, 'gx', 'gy', 'gz')
- migrated: float32 [3, 1341440], P(None, ('gx', 'gy', 'gz'))
- colloid_force: float32 [3, 8192], P(None, ('gx', 'gy', 'gz'))
The draws below stay inside these ranges and needn't reach their ends.
Inputs may be any that keep to these rules, and one draw needn't show every extreme that they name: `grid_shift`: every entry is -1 or 1, and along every dimension the sign changes from each step to the next. `migrate_dir`: code 0 keeps a particle on its device. On every device at most 160 particles take any one nonzero code, and on every device some nonzero code is taken by exactly 160 particles. `migrate_slot`: among the particles of one device with the same nonzero code, the slots are distinct and run from 0 to that code's count minus 1; the slot is 0 where the code is 0. `contact_colloid`: the owner of every contact's colloid is the contact's own device or one of its six face neighbours along gx, gy, gz (periodic).
All inputs are finite; a program needn't handle non-finite values.
Results may differ from the reference program's by a relative error of at most 0.00015.
Values sent between devices are 32-bit elements; how exact they have to be, the bound alone decides.
A program may use at most 128 MiB of HBM per device.

```python
import math
import jax
import jax.numpy as jnp
import numpy as np

CX = 4
CY = 8
CZ = 128
STEPS = 2
COLLOIDS_PER_UNIT = 256
P_DEV = 40960
CAP = 160
CONTACTS_PER_UNIT = 2048
NX = 16
NY = 32
NZ = 256
PARTICLES = 1310720
COLLOIDS = 8192
CONTACTS = 65536
N_GX = 4
N_GY = 4
N_GZ = 2


def draw_grid_shift(key, part):
    signs = 2 * jax.random.randint(jax.random.fold_in(key, 3), (3,), 0, 2) - 1
    flips = jnp.where(jnp.arange(STEPS) % 2 == 0, 1, -1)
    return (flips[:, None] * signs[None, :]).astype(jnp.int32)


def migration_codes(key):
    base = jax.random.fold_in(key, 7)
    device_list = PARTICLES // P_DEV

    def device_codes(device):
        device_key = jax.random.fold_in(base, device)
        key_count, key_forced, key_order = jax.random.split(device_key, 3)
        counts = jax.random.randint(key_count, (6,), CAP // 4, CAP + 1)
        forced = jax.random.randint(key_forced, (), 0, 6)
        counts = jnp.where(jnp.arange(6) == forced, CAP, counts)
        ends = jnp.cumsum(counts)
        starts = ends - counts
        rank = jnp.arange(P_DEV)
        inside = rank < ends[5]
        number = jnp.sum((rank[:, None] >= ends[None, :]).astype(jnp.int32), axis=1)
        codes = jnp.where(inside, 1 + number, 0).astype(jnp.int32)
        places = jnp.where(inside, rank - starts[jnp.clip(number, 0, 5)], 0).astype(jnp.int32)
        order = jax.random.permutation(key_order, P_DEV)
        dirs = jnp.zeros((P_DEV,), jnp.int32).at[order].set(codes)
        slots = jnp.zeros((P_DEV,), jnp.int32).at[order].set(places)
        return (dirs, slots)
    dirs, slots = jax.vmap(device_codes)(jnp.arange(device_list))
    return (dirs.reshape(-1), slots.reshape(-1))


def draw_migrate_dir(key, part):
    return migration_codes(key)[0]


def draw_migrate_slot(key, part):
    return migration_codes(key)[1]


def draw_contact_colloid(key, part):
    grid_x = NX // CX
    grid_y = NY // CY
    grid_z = NZ // CZ
    device_list = grid_x * grid_y * grid_z
    key_near, member_key = jax.random.split(jax.random.fold_in(key, 11))
    neighbour = jax.random.randint(key_near, (device_list, CONTACTS_PER_UNIT), 0, 7)
    member_index = jax.random.randint(member_key, (device_list, CONTACTS_PER_UNIT), 0, COLLOIDS_PER_UNIT)
    moves = jnp.asarray(np.array([[0, 0, 0], [1, 0, 0], [-1, 0, 0], [0, 1, 0], [0, -1, 0], [0, 0, 1], [0, 0, -1]], dtype=np.int32))
    offsets = moves[neighbour]
    device = jnp.arange(device_list, dtype=jnp.int32)[:, None]
    place_x = device // (grid_y * grid_z)
    place_y = device // grid_z % grid_y
    place_z = device % grid_z
    owning_device = ((place_x + offsets[..., 0]) % grid_x * grid_y + (place_y + offsets[..., 1]) % grid_y) * grid_z + (place_z + offsets[..., 2]) % grid_z
    return (owning_device * COLLOIDS_PER_UNIT + member_index).reshape(-1).astype(jnp.int32)


def place_ends(values, own_key, least, high):
    dims = values.shape
    place = [jax.random.randint(jax.random.fold_in(own_key, axis), (), 0, dims[axis]) for axis in range(len(dims))]
    values = values.at[tuple(place)].set(least)
    longest = dims.index(max(dims))
    place[longest] = (place[longest] + 1) % dims[longest]
    return values.at[tuple(place)].set(high)


def block_levels(stream_key, dims, pieces, least, top_value):
    gain = 1.0
    for axis_at, parts in pieces:
        draws = jax.random.uniform(jax.random.fold_in(jax.random.fold_in(stream_key, 6), axis_at), (parts,), jnp.float32, least / len(pieces), top_value / len(pieces))
        gain = gain * jnp.repeat(jnp.exp(draws), dims[axis_at] // parts).reshape((-1,) + (1,) * (len(dims) - 1 - axis_at))
    return gain


def noise(rng, shape, deviation, limit, shards=(), kind=jnp.bfloat16):
    result = deviation * jax.random.normal(rng, shape, jnp.float32)
    if shards:
        result = result * block_levels(rng, shape, shards, -0.22, 0.18)
    return jnp.clip(result, -limit, limit).astype(kind)


def setup_inputs(seed: int = 0) -> dict:
    keys = jax.random.split(jax.random.key(seed), 11)
    velocities = noise(keys[0], (3, PARTICLES), 1.0, 6.0, ((1, 32),), jnp.float32)
    particle_cells = place_ends(jax.random.randint(keys[1], (STEPS, PARTICLES), 0, CX * CY * CZ), jax.random.fold_in(keys[1], 1), 0, (CX * CY * CZ) - 1).astype(jnp.int32)
    grid_shift = draw_grid_shift(jax.random.fold_in(keys[10], 71), 0)
    axis_index = place_ends(jax.random.randint(keys[3], (STEPS, NX, NY, NZ), 0, 8), jax.random.fold_in(keys[3], 1), 0, 7).astype(jnp.int32)
    migrate_dir = draw_migrate_dir(jax.random.fold_in(keys[10], 71), 0)
    migrate_slot = draw_migrate_slot(jax.random.fold_in(keys[10], 71), 0)
    contact_colloid = draw_contact_colloid(jax.random.fold_in(keys[10], 71), 0)
    contact_particle = place_ends(jax.random.randint(keys[7], (CONTACTS,), 0, P_DEV), jax.random.fold_in(keys[7], 1), 0, P_DEV - 1).astype(jnp.int32)
    contact_weight = jnp.clip(jnp.exp(math.log(1.0) - 2.9957323 * jax.random.uniform(keys[8], (CONTACTS,), jnp.float32) ** block_levels(keys[8], (CONTACTS,), ((0, 32),), -0.2, 0.2)), 0.05, 1.0)
    colloid_velocity = noise(keys[9], (3, COLLOIDS), 1.0, 6.0, ((1, 32),), jnp.float32)
    return dict(velocities=velocities, particle_cells=particle_cells, grid_shift=grid_shift, axis_index=axis_index, migrate_dir=migrate_dir, migrate_slot=migrate_slot, contact_colloid=contact_colloid, contact_particle=contact_particle, contact_weight=contact_weight, colloid_velocity=colloid_velocity)


def rotation_table():
    angle = 130.0 * math.pi / 180.0
    cosine = math.cos(angle)
    sine_value = math.sin(angle)
    entries = []
    for number in range(8):
        signs = [1.0 if number >> bit & 1 else -1.0 for bit in range(3)]
        unit = np.array(signs) / math.sqrt(3.0)
        cross = np.array([[0.0, -unit[2], unit[1]], [unit[2], 0.0, -unit[0]], [-unit[1], unit[0], 0.0]])
        matrix = cosine * np.eye(3) + (1.0 - cosine) * np.outer(unit, unit) + sine_value * cross
        entries.append(matrix.reshape(9))
    return np.array(entries)

def cell_rotation(axis_ids, table):
    matrix = jnp.zeros((9,) + axis_ids.shape, jnp.float32)
    for number in range(8):
        chosen = jnp.where(axis_ids == number, 1.0, 0.0).astype(jnp.float32)
        matrix = matrix + chosen[None] * table[number].reshape((9,) + (1,) * axis_ids.ndim)
    return matrix

def apply_rotation(matrix, vector):
    rows = [matrix[3 * row] * vector[0] + matrix[3 * row + 1] * vector[1] + matrix[3 * row + 2] * vector[2] for row in range(3)]
    return jnp.stack(rows)

def reference(velocities, particle_cells, grid_shift, axis_index, migrate_dir, migrate_slot, contact_colloid, contact_particle, contact_weight, colloid_velocity):
    table = jnp.asarray(rotation_table(), jnp.float32)
    cell_total = NX * NY * NZ
    device = (jnp.arange(PARTICLES) // P_DEV).astype(jnp.int32)
    device_x = device // (N_GY * N_GZ)
    device_y = device // N_GZ % N_GY
    device_z = device % N_GZ
    velocity_now = velocities
    mean = jnp.zeros((3, cell_total), jnp.float32)
    for step in range(STEPS):
        local = particle_cells[step]
        cell_x = (device_x * CX + local // (CY * CZ) + grid_shift[step, 0]) % NX
        cell_y = (device_y * CY + local // CZ % CY + grid_shift[step, 1]) % NY
        cell_z = (device_z * CZ + local % CZ + grid_shift[step, 2]) % NZ
        cell = ((cell_x * NY + cell_y) * NZ + cell_z).astype(jnp.int32)
        momentum = jnp.zeros((3, cell_total), jnp.float32).at[:, cell].add(velocity_now)
        counts = jnp.zeros((cell_total,), jnp.float32).at[cell].add(1.0)
        mean = momentum / jnp.maximum(counts, 1.0)
        matrix = cell_rotation(axis_index[step].reshape(-1), table)
        offset = mean - apply_rotation(matrix, mean)
        velocity_now = apply_rotation(matrix[:, cell], velocity_now) + offset[:, cell]
    cell_velocity = mean.reshape(3, NX, NY, NZ)
    device_list = PARTICLES // P_DEV
    leaving = migrate_dir > 0
    target = jnp.where(leaving, device * (6 * CAP) + (migrate_dir - 1) * CAP + migrate_slot, device_list * 6 * CAP).astype(jnp.int32)
    outbox = jnp.zeros((3, device_list * 6 * CAP), jnp.float32).at[:, target].set(velocity_now, mode='drop')
    outbox = outbox.reshape(3, N_GX, N_GY, N_GZ, 6, CAP)
    moves = ((1, 1), (1, -1), (2, 1), (2, -1), (3, 1), (3, -1))
    arrivals = [jnp.roll(outbox[:, :, :, :, number, :], sign, axis=dim) for number, (dim, sign) in enumerate(moves)]
    arrivals = jnp.stack(arrivals, axis=4).reshape(3, device_list, 6 * CAP)
    kept = jnp.where(leaving[None], 0.0, velocity_now).reshape(3, device_list, P_DEV)
    migrated = jnp.concatenate([kept, arrivals], axis=2).reshape(3, device_list * (P_DEV + 6 * CAP))
    contact_device = (jnp.arange(CONTACTS) // CONTACTS_PER_UNIT).astype(jnp.int32)
    particle = (contact_device * P_DEV + contact_particle).astype(jnp.int32)
    weighted = contact_weight[None] * velocity_now[:, particle]
    sum_wv = jnp.zeros((3, COLLOIDS), jnp.float32).at[:, contact_colloid].add(weighted)
    sum_w = jnp.zeros((COLLOIDS,), jnp.float32).at[contact_colloid].add(contact_weight)
    colloid_force = (sum_wv - sum_w * colloid_velocity) / jnp.maximum(sum_w, 1.0)
    return (cell_velocity, migrated, colloid_force)
```

```python
import functools
import math

import jax
import jax.numpy as jnp
from jax import lax
from jax.experimental import pallas as pl
from jax.experimental.pallas import tpu as pltpu
from jax.sharding import PartitionSpec as P

CAP = 160
ANGLE = 130.0 * math.pi / 180.0
COS, SIN = math.cos(ANGLE), math.sin(ANGLE)
TILE = 2048
NT = (((1,), (1,)), ((), ()))
BF = jnp.bfloat16
F32 = jnp.float32


def split_index(c, low):
    if low & (low - 1) == 0:
        return c >> (low.bit_length() - 1), c & (low - 1)
    return c // low, c % low


def one_hot(row, count):
    wide = lax.broadcasted_iota(jnp.int32, (count, row.shape[1]), 0)
    return jnp.where(wide == row, 1.0, 0.0).astype(BF)


def halves(x):
    high = x.astype(BF)
    return high, (x - high.astype(F32)).astype(BF)


def spread(rows, mask):
    return jnp.concatenate([mask * row for row in rows], axis=0)


def hist_tile(c, v, nhi, nlo):
    hi, lo = split_index(c, nlo)
    mask = one_hot(hi, nhi)
    rows = []
    for k in range(3):
        rows.extend(halves(v[k]))
    left = jnp.concatenate([spread(rows, mask), mask], axis=0)
    return lax.dot_general(left, one_hot(lo, nlo), NT, preferred_element_type=F32)


def mean_of(acc, mean_ref, nhi):
    count = jnp.maximum(acc[6 * nhi : 7 * nhi], 1.0)
    for k in range(3):
        total = acc[2 * k * nhi : (2 * k + 1) * nhi] + acc[(2 * k + 1) * nhi : (2 * k + 2) * nhi]
        mean_ref[k] = total / count


def signs_of(index):
    return [jnp.where((index & (1 << i)) != 0, 1.0, -1.0) for i in range(3)]


def rotate(e, v):
    along = ((1.0 - COS) / 3.0) * (e[0] * v[0] + e[1] * v[1] + e[2] * v[2])
    turn = SIN / math.sqrt(3.0)
    out = []
    for i in range(3):
        j, k = (i + 1) % 3, (i + 2) % 3
        out.append(COS * v[i] + e[i] * along + turn * (e[j] * v[k] - e[k] * v[j]))
    return out


def make_table(mean_ref, axis_ref, table_ref, nhi, nlo):
    mean = [mean_ref[k] for k in range(3)]
    index = axis_ref[...]
    turned = rotate(signs_of(index), mean)
    for k in range(3):
        high, low = halves(mean[k] - turned[k])
        table_ref[k * nhi : (k + 1) * nhi, 0:nlo] = high
        table_ref[k * nhi : (k + 1) * nhi, nlo : 2 * nlo] = low
    table_ref[3 * nhi : 4 * nhi, 0:nlo] = index.astype(F32).astype(BF)
    table_ref[3 * nhi : 4 * nhi, nlo : 2 * nlo] = jnp.zeros((nhi, nlo), BF)


def collide_tile(c, v, table, nhi, nlo):
    hi, lo = split_index(c, nlo)
    hot = one_hot(lo, nlo)
    got = jnp.dot(table, jnp.concatenate([hot, hot], axis=0), preferred_element_type=F32)
    here = lax.broadcasted_iota(jnp.int32, (nhi, c.shape[1]), 0) == hi
    picked = [
        jnp.sum(jnp.where(here, got[q * nhi : (q + 1) * nhi], 0.0), axis=0, keepdims=True)
        for q in range(4)
    ]
    turned = rotate(signs_of(picked[3].astype(jnp.int32)), v)
    return [turned[k] + picked[k] for k in range(3)]


def rows3(ref, at):
    return [ref[k : k + 1, at] for k in range(3)]


def first_kernel(tile, nhi, nlo, cell_ref, v_ref, mean_ref, acc):
    acc[...] = jnp.zeros_like(acc)

    def step(t, carry):
        at = pl.ds(pl.multiple_of(t * tile, tile), tile)
        acc[...] += hist_tile(cell_ref[0:1, at], rows3(v_ref, at), nhi, nlo)
        return carry

    lax.fori_loop(0, v_ref.shape[1] // tile, step, 0)
    mean_of(acc, mean_ref, nhi)


def middle_kernel(
    tile, nhi, nlo, cell_ref, v_ref, mean_ref, axis_ref, next_ref, next_mean_ref, acc, table_ref
):
    acc[...] = jnp.zeros_like(acc)
    make_table(mean_ref, axis_ref, table_ref, nhi, nlo)

    def step(t, carry):
        at = pl.ds(pl.multiple_of(t * tile, tile), tile)
        new = collide_tile(cell_ref[0:1, at], rows3(v_ref, at), table_ref[...], nhi, nlo)
        for k in range(3):
            next_ref[k : k + 1, at] = new[k]
        acc[...] += hist_tile(cell_ref[1:2, at], new, nhi, nlo)
        return carry

    lax.fori_loop(0, v_ref.shape[1] // tile, step, 0)
    mean_of(acc, next_mean_ref, nhi)


def last_kernel(
    tile, nhi, nlo, units, cell_ref, v_ref, mean_ref, axis_ref, dir_ref, slot_ref, place_ref, who_ref,
    weight_ref, kept_ref, o0, o1, o2, o3, o4, o5, own_ref, moved, table_ref, seen
):
    moved[...] = jnp.zeros_like(moved)
    make_table(mean_ref, axis_ref, table_ref, nhi, nlo)
    per = tile // 128

    def step(t, carry):
        at = pl.ds(pl.multiple_of(t * tile, tile), tile)
        new = collide_tile(cell_ref[1:2, at], rows3(v_ref, at), table_ref[...], nhi, nlo)
        code = dir_ref[0:1, at]
        stays = code == 0
        rows = []
        for k in range(3):
            kept_ref[k : k + 1, at] = jnp.where(stays, new[k], 0.0)
            rows.extend(halves(new[k]))
            for j in range(per):
                seen[k, pl.ds(t * per + j, 1), :] = new[k][:, j * 128 : (j + 1) * 128]
        mask = one_hot(code - 1, 16)
        moved[...] += lax.dot_general(
            spread(rows, mask), one_hot(slot_ref[0:1, at], CAP), NT, preferred_element_type=F32
        )
        return carry

    lax.fori_loop(0, v_ref.shape[1] // tile, step, 0)

    contacts = who_ref.shape[1]
    chunk = min(512, contacts)
    groups = seen.shape[1]
    sums = jnp.zeros((8 * 16, units), F32)
    parts = [halves(seen[k]) for k in range(3)]
    book = jnp.concatenate([jnp.concatenate(p, axis=1) for p in parts], axis=0)
    for c in range(contacts // chunk):
        at = slice(c * chunk, (c + 1) * chunk)
        hi, lo = split_index(who_ref[0:1, at], 128)
        hot = one_hot(lo, 128)
        got = jnp.dot(book, jnp.concatenate([hot, hot], axis=0), preferred_element_type=F32)
        here = lax.broadcasted_iota(jnp.int32, (groups, chunk), 0) == hi
        weight = weight_ref[0:1, at]
        rows = []
        for k in range(3):
            mine = jnp.where(here, got[k * groups : (k + 1) * groups], 0.0)
            rows.extend(halves(weight * jnp.sum(mine, axis=0, keepdims=True)))
        rows.extend(halves(weight))
        code, member = split_index(place_ref[0:1, at], units)
        sums = sums + lax.dot_general(
            spread(rows, one_hot(code, 16)), one_hot(member, units), NT, preferred_element_type=F32
        )
    totals = [sums[32 * k : 32 * k + 16] + sums[32 * k + 16 : 32 * k + 32] for k in range(4)]
    own_ref[...] = jnp.concatenate([t[6:7] for t in totals], axis=0)
    for d, out in enumerate((o0, o1, o2, o3, o4, o5)):
        out[...] = jnp.zeros_like(out)
        for k in range(3):
            out[k : k + 1, 0:CAP] = (
                moved[32 * k + d : 32 * k + d + 1] + moved[32 * k + 16 + d : 32 * k + 17 + d]
            )
        for k in range(4):
            out[4 + k : 5 + k, 0:units] = totals[k][d : d + 1]


def ring(axis, sign):
    count = lax.axis_size(axis)
    return [(i, (i + sign) % count) for i in range(count)]


def take(x, dim, where):
    start = x.shape[dim] - 1 if where < 0 else 0
    return lax.slice_in_dim(x, start, start + 1, axis=dim)


def pulled(x, dim, face, sign):
    size = x.shape[dim]
    if sign > 0:
        return jnp.concatenate([lax.slice_in_dim(x, 1, size, axis=dim), face], axis=dim)
    return jnp.concatenate([face, lax.slice_in_dim(x, 0, size - 1, axis=dim)], axis=dim)


def axis_tables(axis_index, grid_shift):
    first, second = axis_index[0], axis_index[1]
    for dim, axis in enumerate(("gx", "gy", "gz")):
        up = grid_shift[0, dim] > 0
        plus, minus = jnp.where(up, first, second), jnp.where(up, second, first)
        after = lax.ppermute(take(plus, dim, 0), axis, ring(axis, -1))
        before = lax.ppermute(take(minus, dim, -1), axis, ring(axis, 1))
        plus, minus = pulled(plus, dim, after, 1), pulled(minus, dim, before, -1)
        first, second = jnp.where(up, plus, minus), jnp.where(up, minus, plus)
    return first, second


def placed_mean(mean, shift):
    for dim, axis in enumerate(("gx", "gy", "gz")):
        d = dim + 1
        after = lax.ppermute(take(mean, d, 0), axis, ring(axis, -1))
        before = lax.ppermute(take(mean, d, -1), axis, ring(axis, 1))
        mean = jnp.where(shift[dim] > 0, pulled(mean, d, before, -1), pulled(mean, d, after, 1))
    return mean


def contact_places(contact_colloid, units):
    size_x, size_y, size_z = (lax.axis_size(a) for a in ("gx", "gy", "gz"))
    mine_x, mine_y, mine_z = (lax.axis_index(a) for a in ("gx", "gy", "gz"))
    owner = contact_colloid // units
    apart_x = (owner // (size_y * size_z) - mine_x) % size_x
    apart_y = (owner // size_z % size_y - mine_y) % size_y
    apart_z = (owner % size_z - mine_z) % size_z
    code = jnp.full(owner.shape, 6, jnp.int32)
    for number, (apart, to) in reversed(
        list(
            enumerate(
                (
                    (apart_x, 1), (apart_x, size_x - 1), (apart_y, 1),
                    (apart_y, size_y - 1), (apart_z, 1), (apart_z, size_z - 1),
                )
            )
        )
    ):
        code = jnp.where(apart == to, number, code)
    return code * units + contact_colloid % units


def body(
    velocities, particle_cells, grid_shift, axis_index, migrate_dir, migrate_slot,
    contact_colloid, contact_particle, contact_weight, colloid_velocity,
):
    _, cx, cy, nlo = axis_index.shape
    nhi = cx * cy
    particles = velocities.shape[1]
    units = colloid_velocity.shape[1]
    tile = math.gcd(particles, TILE)
    mean_shape = jax.ShapeDtypeStruct((3, nhi, nlo), F32)
    acc = pltpu.VMEM((7 * nhi, nlo), F32)
    table = pltpu.VMEM((4 * nhi, 2 * nlo), BF)
    params = pltpu.CompilerParams(vmem_limit_bytes=48 * 2**20)
    vmem = pl.BlockSpec(memory_space=pltpu.VMEM)

    def call(kernel, outs, scratch, flops, *args):
        many = isinstance(outs, tuple)
        return pl.pallas_call(
            functools.partial(kernel, tile, nhi, nlo),
            out_shape=outs,
            in_specs=[vmem] * len(args),
            out_specs=tuple([vmem] * len(outs)) if many else vmem,
            scratch_shapes=scratch,
            compiler_params=params,
            cost_estimate=pl.CostEstimate(flops=flops, bytes_accessed=30_000_000, transcendentals=0),
        )(*args)

    places = contact_places(contact_colloid, units)
    axis0, axis1 = axis_tables(axis_index, grid_shift)
    mean0 = call(first_kernel, mean_shape, [acc], 10**9, particle_cells, velocities)
    v1, mean1 = call(
        middle_kernel, (jax.ShapeDtypeStruct(velocities.shape, F32), mean_shape), [acc, table], 10**9,
        particle_cells, velocities, mean0, axis0.reshape(nhi, nlo),
    )
    box = jax.ShapeDtypeStruct((8, max(units, 256)), F32)
    outs = call(
        lambda t, h, l, *refs: last_kernel(t, h, l, units, *refs),
        (jax.ShapeDtypeStruct((3, particles + 6 * CAP), F32),)
        + (box,) * 6
        + (jax.ShapeDtypeStruct((4, units), F32),),
        [pltpu.VMEM((96, CAP), F32), table, pltpu.VMEM((3, particles // 128, 128), F32)],
        10**9,
        particle_cells, v1, mean1, axis1.reshape(nhi, nlo), migrate_dir.reshape(1, -1),
        migrate_slot.reshape(1, -1), places.reshape(1, -1), contact_particle.reshape(1, -1),
        contact_weight.reshape(1, -1),
    )
    cell_velocity = placed_mean(mean1.reshape(3, cx, cy, nlo), grid_shift[axis_index.shape[0] - 1])
    arrived = [
        lax.ppermute(outs[1 + d], ("gx", "gy", "gz")[d // 2], ring(("gx", "gy", "gz")[d // 2], 1 - 2 * (d % 2)))
        for d in range(6)
    ]
    tail = jnp.concatenate([a[0:3, 0:CAP] for a in arrived], axis=1)
    migrated = lax.dynamic_update_slice(outs[0], tail, (0, particles))
    total = outs[7]
    for a in arrived:
        total = total + a[4:8, 0:units]
    sum_w = total[3:4]
    force = (total[0:3] - sum_w * colloid_velocity) / jnp.maximum(sum_w, 1.0)
    return (cell_velocity, migrated, force)


def solution(mesh):
    flat = P(None, ("gx", "gy", "gz"))
    line = P(("gx", "gy", "gz"))
    grid = P(None, "gx", "gy", "gz")
    return jax.shard_map(
        body,
        mesh=mesh,
        in_specs=(flat, flat, P(), grid, line, line, line, line, line, flat),
        out_specs=(grid, flat, flat),
        check_vma=False,
    )
```

```python
import functools
import math

import jax
import jax.numpy as jnp
from jax import lax
from jax.experimental import pallas as pl
from jax.experimental.pallas import tpu as pltpu
from jax.sharding import PartitionSpec as P

CAP = 160
ANGLE = 130.0 * math.pi / 180.0
COS, SIN = math.cos(ANGLE), math.sin(ANGLE)
TILE = 2048
NT = (((1,), (1,)), ((), ()))
BF = jnp.bfloat16
F32 = jnp.float32


def split_index(c, low):
    if low & (low - 1) == 0:
        return c >> (low.bit_length() - 1), c & (low - 1)
    return c // low, c % low


def one_hot(row, count):
    wide = lax.broadcasted_iota(jnp.int32, (count, row.shape[1]), 0)
    return jnp.where(wide == row, 1.0, 0.0).astype(BF)


def halves(x):
    high = x.astype(BF)
    return high, (x - high.astype(F32)).astype(BF)


def spread(rows, mask):
    return jnp.concatenate([mask * row for row in rows], axis=0)


def hist_tile(c, v, nhi, nlo):
    hi, lo = split_index(c, nlo)
    mask = one_hot(hi, nhi)
    rows = []
    for k in range(3):
        rows.extend(halves(v[k]))
    left = jnp.concatenate([spread(rows, mask), mask], axis=0)
    return lax.dot_general(left, one_hot(lo, nlo), NT, preferred_element_type=F32)


def mean_of(acc, mean_ref, nhi):
    count = jnp.maximum(acc[6 * nhi : 7 * nhi], 1.0)
    for k in range(3):
        total = acc[2 * k * nhi : (2 * k + 1) * nhi] + acc[(2 * k + 1) * nhi : (2 * k + 2) * nhi]
        mean_ref[k] = total / count


def signs_of(index):
    return [jnp.where((index & (1 << i)) != 0, 1.0, -1.0) for i in range(3)]


def rotate(e, v):
    along = ((1.0 - COS) / 3.0) * (e[0] * v[0] + e[1] * v[1] + e[2] * v[2])
    turn = SIN / math.sqrt(3.0)
    out = []
    for i in range(3):
        j, k = (i + 1) % 3, (i + 2) % 3
        out.append(COS * v[i] + e[i] * along + turn * (e[j] * v[k] - e[k] * v[j]))
    return out


def make_table(mean_ref, axis_ref, table_ref, nhi, nlo):
    mean = [mean_ref[k] for k in range(3)]
    index = axis_ref[...]
    turned = rotate(signs_of(index), mean)
    for k in range(3):
        high, low = halves(mean[k] - turned[k])
        table_ref[k * nhi : (k + 1) * nhi, 0:nlo] = high
        table_ref[k * nhi : (k + 1) * nhi, nlo : 2 * nlo] = low
    table_ref[3 * nhi : 4 * nhi, 0:nlo] = index.astype(F32).astype(BF)
    table_ref[3 * nhi : 4 * nhi, nlo : 2 * nlo] = jnp.zeros((nhi, nlo), BF)


def collide_tile(c, v, table, nhi, nlo):
    hi, lo = split_index(c, nlo)
    hot = one_hot(lo, nlo)
    got = jnp.dot(table, jnp.concatenate([hot, hot], axis=0), preferred_element_type=F32)
    here = lax.broadcasted_iota(jnp.int32, (nhi, c.shape[1]), 0) == hi
    picked = [
        jnp.sum(jnp.where(here, got[q * nhi : (q + 1) * nhi], 0.0), axis=0, keepdims=True)
        for q in range(4)
    ]
    turned = rotate(signs_of(picked[3].astype(jnp.int32)), v)
    return [turned[k] + picked[k] for k in range(3)]


def rows3(ref, at):
    return [ref[k : k + 1, at] for k in range(3)]


def first_kernel(tile, nhi, nlo, cell_ref, v_ref, mean_ref, acc):
    acc[...] = jnp.zeros_like(acc)

    def step(t, carry):
        at = pl.ds(pl.multiple_of(t * tile, tile), tile)
        acc[...] += hist_tile(cell_ref[0:1, at], rows3(v_ref, at), nhi, nlo)
        return carry

    lax.fori_loop(0, v_ref.shape[1] // tile, step, 0)
    mean_of(acc, mean_ref, nhi)


def middle_kernel(
    tile, nhi, nlo, cell_ref, v_ref, mean_ref, axis_ref, next_ref, next_mean_ref, acc, table_ref
):
    acc[...] = jnp.zeros_like(acc)
    make_table(mean_ref, axis_ref, table_ref, nhi, nlo)

    def step(t, carry):
        at = pl.ds(pl.multiple_of(t * tile, tile), tile)
        new = collide_tile(cell_ref[0:1, at], rows3(v_ref, at), table_ref[...], nhi, nlo)
        for k in range(3):
            next_ref[k : k + 1, at] = new[k]
        acc[...] += hist_tile(cell_ref[1:2, at], new, nhi, nlo)
        return carry

    lax.fori_loop(0, v_ref.shape[1] // tile, step, 0)
    mean_of(acc, next_mean_ref, nhi)


def last_kernel(
    tile, nhi, nlo, units, cell_ref, v_ref, mean_ref, axis_ref, dir_ref, slot_ref, place_ref, who_ref,
    weight_ref, kept_ref, o0, o1, o2, o3, o4, o5, own_ref, moved, table_ref, seen
):
    moved[...] = jnp.zeros_like(moved)
    make_table(mean_ref, axis_ref, table_ref, nhi, nlo)
    per = tile // 128

    def step(t, carry):
        at = pl.ds(pl.multiple_of(t * tile, tile), tile)
        new = collide_tile(cell_ref[1:2, at], rows3(v_ref, at), table_ref[...], nhi, nlo)
        code = dir_ref[0:1, at]
        stays = code == 0
        rows = []
        for k in range(3):
            kept_ref[k : k + 1, at] = jnp.where(stays, new[k], 0.0)
            rows.extend(halves(new[k]))
            for j in range(per):
                seen[k, pl.ds(t * per + j, 1), :] = new[k][:, j * 128 : (j + 1) * 128]
        mask = one_hot(code - 1, 16)
        moved[...] += lax.dot_general(
            spread(rows, mask), one_hot(slot_ref[0:1, at], CAP), NT, preferred_element_type=F32
        )
        return carry

    lax.fori_loop(0, v_ref.shape[1] // tile, step, 0)

    contacts = who_ref.shape[1]
    chunk = min(512, contacts)
    groups = seen.shape[1]
    sums = jnp.zeros((8 * 16, units), F32)
    parts = [halves(seen[k]) for k in range(3)]
    book = jnp.concatenate([jnp.concatenate(p, axis=1) for p in parts], axis=0)
    for c in range(contacts // chunk):
        at = slice(c * chunk, (c + 1) * chunk)
        hi, lo = split_index(who_ref[0:1, at], 128)
        hot = one_hot(lo, 128)
        got = jnp.dot(book, jnp.concatenate([hot, hot], axis=0), preferred_element_type=F32)
        here = lax.broadcasted_iota(jnp.int32, (groups, chunk), 0) == hi
        weight = weight_ref[0:1, at]
        rows = []
        for k in range(3):
            mine = jnp.where(here, got[k * groups : (k + 1) * groups], 0.0)
            rows.extend(halves(weight * jnp.sum(mine, axis=0, keepdims=True)))
        rows.extend(halves(weight))
        code, member = split_index(place_ref[0:1, at], units)
        sums = sums + lax.dot_general(
            spread(rows, one_hot(code, 16)), one_hot(member, units), NT, preferred_element_type=F32
        )
    totals = [sums[32 * k : 32 * k + 16] + sums[32 * k + 16 : 32 * k + 32] for k in range(4)]
    own_ref[...] = jnp.concatenate([t[6:7] for t in totals], axis=0)
    for d, out in enumerate((o0, o1, o2, o3, o4, o5)):
        out[...] = jnp.zeros_like(out)
        for k in range(3):
            out[k : k + 1, 0:CAP] = (
                moved[32 * k + d : 32 * k + d + 1] + moved[32 * k + 16 + d : 32 * k + 17 + d]
            )
        for k in range(4):
            out[4 + k : 5 + k, 0:units] = totals[k][d : d + 1]


AXES = ("gx", "gy", "gz")
MESH = pl.DeviceIdType.MESH


def beside(axis, sign):
    count = lax.axis_size(axis)
    return {axis: lax.rem(lax.axis_index(axis) + (sign + count), count)}


def greet():
    barrier = pltpu.get_barrier_semaphore()
    for axis in AXES:
        for sign in (1, -1):
            pl.semaphore_signal(barrier, inc=1, device_id=beside(axis, sign), device_id_type=MESH)
    pl.semaphore_wait(barrier, 6)


def send(src, dst, sems, number, axis, sign):
    copy = pltpu.make_async_remote_copy(
        src_ref=src, dst_ref=dst, send_sem=sems[0].at[number], recv_sem=sems[1].at[number],
        device_id=beside(axis, sign), device_id_type=MESH,
    )
    copy.start()
    return copy


def both(pair, box, sems, number, axis):
    return [
        send(pair[0], box.at[0], sems, number, axis, -1),
        send(pair[1], box.at[1], sems, number + 1, axis, 1),
    ]


def shift_fields(rows, flip, shift_ref, x_ref, put, zbox, xbox, ybox, work, faces, sems, first):
    n, cx, cy, nz = x_ref.shape
    ups = [[shift_ref[r, dim] * flip > 0 for dim in range(3)] for r in rows]
    for copy in both((x_ref, x_ref), zbox, sems, first, "gz"):
        copy.wait()
    for f in range(n):
        x = x_ref[f]
        plus = jnp.concatenate([x[:, :, 1:], zbox[0, f][:, :, 0:1]], axis=2)
        minus = jnp.concatenate([zbox[1, f][:, :, nz - 1 :], x[:, :, : nz - 1]], axis=2)
        work[f] = jnp.where(ups[f][2], plus, minus)
    for copy in both((work.at[:, 0], work.at[:, cx - 1]), xbox, sems, first + 2, "gx"):
        copy.wait()
    held = []
    for f in range(n):
        x = work[f]
        plus = [x[i] for i in range(1, cx)] + [xbox[0, f]]
        minus = [xbox[1, f]] + [x[i] for i in range(cx - 1)]
        held.append([jnp.where(ups[f][0], p, m) for p, m in zip(plus, minus)])
        for i in range(cx):
            faces[0, f, i : i + 1, :] = held[f][i][0:1]
            faces[1, f, i : i + 1, :] = held[f][i][cy - 1 :]
    for copy in both((faces.at[0], faces.at[1]), ybox, sems, first + 4, "gy"):
        copy.wait()
    for f in range(n):
        for i in range(cx):
            x = held[f][i]
            plus = jnp.concatenate([x[1:], ybox[0, f, i : i + 1, :]], axis=0)
            minus = jnp.concatenate([ybox[1, f, i : i + 1, :], x[: cy - 1]], axis=0)
            put(f, i, jnp.where(ups[f][1], plus, minus))


def shift_scratch(shape, kind):
    n, cx, cy, nz = shape
    return [
        pltpu.VMEM((2, n, cx, cy, nz), kind), pltpu.VMEM((2, n, cy, nz), kind),
        pltpu.VMEM((2, n, cx, nz), kind), pltpu.VMEM((n, cx, cy, nz), kind),
        pltpu.VMEM((2, n, cx, nz), kind),
    ]


def axis_kernel(shift_ref, x_ref, out_ref, zbox, xbox, ybox, work, faces, out_sem, in_sem):
    greet()

    def put(f, i, value):
        out_ref[f, i] = value

    rows = list(range(x_ref.shape[0]))
    shift_fields(
        rows, 1, shift_ref, x_ref, put, zbox, xbox, ybox, work, faces, (out_sem, in_sem), 0
    )


def tail_kernel(
    units, shift_ref, x_ref, b0, b1, b2, b3, b4, b5, own_ref, drift_ref, out_ref, tail_ref, force_ref,
    zbox, xbox, ybox, work, faces, arrived, out_sem, in_sem
):
    greet()
    sems = (out_sem, in_sem)
    copies = [
        send(b, arrived.at[d], sems, 6 + d, AXES[d // 2], 1 - 2 * (d % 2))
        for d, b in enumerate((b0, b1, b2, b3, b4, b5))
    ]

    def put(f, i, value):
        out_ref[f, i] = value

    rows = [shift_ref.shape[0] - 1] * x_ref.shape[0]
    shift_fields(rows, -1, shift_ref, x_ref, put, zbox, xbox, ybox, work, faces, sems, 0)
    total = own_ref[...]
    for d, copy in enumerate(copies):
        copy.wait()
        tail_ref[:, d * CAP : (d + 1) * CAP] = arrived[d, 0:3, 0:CAP]
        total = total + arrived[d, 4:8, 0:units]
    sum_w = total[3:4]
    force_ref[...] = (total[0:3] - sum_w * drift_ref[...]) / jnp.maximum(sum_w, 1.0)


def contact_places(contact_colloid, units):
    size_x, size_y, size_z = (lax.axis_size(a) for a in ("gx", "gy", "gz"))
    mine_x, mine_y, mine_z = (lax.axis_index(a) for a in ("gx", "gy", "gz"))
    owner = contact_colloid // units
    apart_x = (owner // (size_y * size_z) - mine_x) % size_x
    apart_y = (owner // size_z % size_y - mine_y) % size_y
    apart_z = (owner % size_z - mine_z) % size_z
    code = jnp.full(owner.shape, 6, jnp.int32)
    for number, (apart, to) in reversed(
        list(
            enumerate(
                (
                    (apart_x, 1), (apart_x, size_x - 1), (apart_y, 1),
                    (apart_y, size_y - 1), (apart_z, 1), (apart_z, size_z - 1),
                )
            )
        )
    ):
        code = jnp.where(apart == to, number, code)
    return code * units + contact_colloid % units


def body(
    velocities, particle_cells, grid_shift, axis_index, migrate_dir, migrate_slot,
    contact_colloid, contact_particle, contact_weight, colloid_velocity,
):
    _, cx, cy, nlo = axis_index.shape
    nhi = cx * cy
    particles = velocities.shape[1]
    units = colloid_velocity.shape[1]
    tile = math.gcd(particles, TILE)
    mean_shape = jax.ShapeDtypeStruct((3, nhi, nlo), F32)
    acc = pltpu.VMEM((7 * nhi, nlo), F32)
    table = pltpu.VMEM((4 * nhi, 2 * nlo), BF)
    params = pltpu.CompilerParams(vmem_limit_bytes=48 * 2**20)
    vmem = pl.BlockSpec(memory_space=pltpu.VMEM)

    def call(kernel, outs, scratch, flops, *args):
        many = isinstance(outs, tuple)
        return pl.pallas_call(
            functools.partial(kernel, tile, nhi, nlo),
            out_shape=outs,
            in_specs=[vmem] * len(args),
            out_specs=tuple([vmem] * len(outs)) if many else vmem,
            scratch_shapes=scratch,
            compiler_params=params,
            cost_estimate=pl.CostEstimate(flops=flops, bytes_accessed=30_000_000, transcendentals=0),
        )(*args)

    places = contact_places(contact_colloid, units)
    smem = pl.BlockSpec(memory_space=pltpu.SMEM)
    turned = pl.pallas_call(
        axis_kernel,
        out_shape=jax.ShapeDtypeStruct(axis_index.shape, jnp.int32),
        in_specs=[smem, vmem],
        out_specs=vmem,
        scratch_shapes=shift_scratch(axis_index.shape, jnp.int32)
        + [pltpu.SemaphoreType.DMA((6,)), pltpu.SemaphoreType.DMA((6,))],
        compiler_params=pltpu.CompilerParams(collective_id=0, has_side_effects=True),
    )(grid_shift, axis_index)
    axis0, axis1 = turned[0], turned[1]
    mean0 = call(first_kernel, mean_shape, [acc], 10**9, particle_cells, velocities)
    v1, mean1 = call(
        middle_kernel, (jax.ShapeDtypeStruct(velocities.shape, F32), mean_shape), [acc, table], 10**9,
        particle_cells, velocities, mean0, axis0.reshape(nhi, nlo),
    )
    box = jax.ShapeDtypeStruct((8, max(units, 256)), F32)
    outs = call(
        lambda t, h, l, *refs: last_kernel(t, h, l, units, *refs),
        (jax.ShapeDtypeStruct((3, particles + 6 * CAP), F32),)
        + (box,) * 6
        + (jax.ShapeDtypeStruct((4, units), F32),),
        [pltpu.VMEM((96, CAP), F32), table, pltpu.VMEM((3, particles // 128, 128), F32)],
        10**9,
        particle_cells, v1, mean1, axis1.reshape(nhi, nlo), migrate_dir.reshape(1, -1),
        migrate_slot.reshape(1, -1), places.reshape(1, -1), contact_particle.reshape(1, -1),
        contact_weight.reshape(1, -1),
    )
    mean_box = mean1.reshape(3, cx, cy, nlo)
    cell_velocity, tail, force = pl.pallas_call(
        functools.partial(tail_kernel, units),
        out_shape=(
            jax.ShapeDtypeStruct(mean_box.shape, F32),
            jax.ShapeDtypeStruct((3, 6 * CAP), F32),
            jax.ShapeDtypeStruct((3, units), F32),
        ),
        in_specs=[smem] + [vmem] * 9,
        out_specs=(vmem, vmem, vmem),
        scratch_shapes=shift_scratch(mean_box.shape, F32)
        + [pltpu.VMEM((6,) + box.shape, F32)]
        + [pltpu.SemaphoreType.DMA((12,)), pltpu.SemaphoreType.DMA((12,))],
        compiler_params=pltpu.CompilerParams(collective_id=1, has_side_effects=True),
    )(grid_shift, mean_box, *outs[1:8], colloid_velocity)
    migrated = lax.dynamic_update_slice(outs[0], tail, (0, particles))
    return (cell_velocity, migrated, force)


def solution(mesh):
    flat = P(None, ("gx", "gy", "gz"))
    line = P(("gx", "gy", "gz"))
    grid = P(None, "gx", "gy", "gz")
    return jax.shard_map(
        body,
        mesh=mesh,
        in_specs=(flat, flat, P(), grid, line, line, line, line, line, flat),
        out_specs=(grid, flat, flat),
        check_vma=False,
    )
```

```python
import functools
import math

import jax
import jax.numpy as jnp
from jax import lax
from jax.experimental import pallas as pl
from jax.experimental.pallas import tpu as pltpu
from jax.sharding import PartitionSpec as P

CAP = 160
ANGLE = 130.0 * math.pi / 180.0
COS, SIN = math.cos(ANGLE), math.sin(ANGLE)
TILE = 2048
NT = (((1,), (1,)), ((), ()))
BF = jnp.bfloat16
F32 = jnp.float32


def split_index(c, low):
    if low & (low - 1) == 0:
        return c >> (low.bit_length() - 1), c & (low - 1)
    return c // low, c % low


def one_hot(row, count):
    kind = BF if count <= 256 else F32
    wide = lax.broadcasted_iota(jnp.int32, (count, row.shape[1]), 0).astype(F32).astype(kind)
    return jnp.where(wide == row.astype(F32).astype(kind), jnp.ones((), kind), jnp.zeros((), kind)).astype(BF)


def halves(x):
    high = x.astype(BF)
    return high, (x - high.astype(F32)).astype(BF)


def spread(rows, mask):
    return jnp.concatenate([mask * row for row in rows], axis=0)


def hist_tile(c, v, nhi, nlo):
    hi, lo = split_index(c, nlo)
    mask = one_hot(hi, nhi)
    rows = []
    for k in range(3):
        rows.extend(halves(v[k]))
    left = jnp.concatenate([spread(rows, mask), mask], axis=0)
    return lax.dot_general(left, one_hot(lo, nlo), NT, preferred_element_type=F32)


def mean_of(acc, mean_ref, nhi):
    count = jnp.maximum(acc[6 * nhi : 7 * nhi], 1.0)
    for k in range(3):
        total = acc[2 * k * nhi : (2 * k + 1) * nhi] + acc[(2 * k + 1) * nhi : (2 * k + 2) * nhi]
        mean_ref[k] = total / count


def signs_of(index):
    return [jnp.where((index & (1 << i)) != 0, 1.0, -1.0) for i in range(3)]


def rotate(e, v):
    along = ((1.0 - COS) / 3.0) * (e[0] * v[0] + e[1] * v[1] + e[2] * v[2])
    turn = SIN / math.sqrt(3.0)
    out = []
    for i in range(3):
        j, k = (i + 1) % 3, (i + 2) % 3
        out.append(COS * v[i] + e[i] * along + turn * (e[j] * v[k] - e[k] * v[j]))
    return out


def make_table(mean_ref, axis_ref, table_ref, nhi, nlo):
    mean = [mean_ref[k] for k in range(3)]
    index = axis_ref[...]
    turned = rotate(signs_of(index), mean)
    for k in range(3):
        high, low = halves(mean[k] - turned[k])
        table_ref[k * nhi : (k + 1) * nhi, 0:nlo] = high
        table_ref[k * nhi : (k + 1) * nhi, nlo : 2 * nlo] = low
    table_ref[3 * nhi : 4 * nhi, 0:nlo] = index.astype(F32).astype(BF)
    table_ref[3 * nhi : 4 * nhi, nlo : 2 * nlo] = jnp.zeros((nhi, nlo), BF)


def collide_tile(c, v, table, nhi, nlo):
    hi, lo = split_index(c, nlo)
    hot = one_hot(lo, nlo)
    got = jnp.dot(table, jnp.concatenate([hot, hot], axis=0), preferred_element_type=F32)
    here = lax.broadcasted_iota(jnp.int32, (nhi, c.shape[1]), 0) == hi
    picked = [
        jnp.sum(jnp.where(here, got[q * nhi : (q + 1) * nhi], 0.0), axis=0, keepdims=True)
        for q in range(4)
    ]
    turned = rotate(signs_of(picked[3].astype(jnp.int32)), v)
    return [turned[k] + picked[k] for k in range(3)]


def rows3(ref, at):
    return [ref[k : k + 1, at] for k in range(3)]


def first_kernel(
    tile, nhi, nlo, shift_ref, x_ref, cell_ref, v_ref, mean_ref, axis0_ref, axis1_ref,
    acc, zbox, xbox, ybox, work, turned, faces, out_sem, in_sem
):
    acc[...] = jnp.zeros_like(acc)
    cy = x_ref.shape[2]

    def put(f, i, value):
        (axis0_ref, axis1_ref)[f][i * cy : (i + 1) * cy, :] = value

    def step(t, carry):
        at = pl.ds(pl.multiple_of(t * tile, tile), tile)
        acc[...] += hist_tile(cell_ref[0:1, at], rows3(v_ref, at), nhi, nlo)
        return carry

    transfer = shift_fields(
        (0, 1), 1, shift_ref, x_ref, put, zbox, xbox, ybox, work, turned, faces, (out_sem, in_sem)
    )
    beside_work(transfer, step, v_ref.shape[1] // tile)
    mean_of(acc, mean_ref, nhi)


def middle_kernel(
    tile, nhi, nlo, cell_ref, v_ref, mean_ref, axis_ref, next_ref, next_mean_ref, acc, table_ref
):
    acc[...] = jnp.zeros_like(acc)
    make_table(mean_ref, axis_ref, table_ref, nhi, nlo)

    def step(t, carry):
        at = pl.ds(pl.multiple_of(t * tile, tile), tile)
        new = collide_tile(cell_ref[0:1, at], rows3(v_ref, at), table_ref[...], nhi, nlo)
        for k in range(3):
            next_ref[k : k + 1, at] = new[k]
        acc[...] += hist_tile(cell_ref[1:2, at], new, nhi, nlo)
        return carry

    lax.fori_loop(0, v_ref.shape[1] // tile, step, 0)
    mean_of(acc, next_mean_ref, nhi)


def last_kernel(
    tile, nhi, nlo, units, shift_ref, x_ref, cell_ref, v_ref, mean_ref, axis_ref, dir_ref, slot_ref,
    place_ref, who_ref, weight_ref, drift_ref, out_ref, kept_ref, force_ref, moved, table_ref, seen,
    going, coming, pushes, pulls, zbox, xbox, ybox, work, turned, faces, out_sem, in_sem
):
    moved[...] = jnp.zeros_like(moved)
    make_table(mean_ref, axis_ref, table_ref, nhi, nlo)
    per = tile // 128

    def step(t, carry):
        at = pl.ds(pl.multiple_of(t * tile, tile), tile)
        new = collide_tile(cell_ref[1:2, at], rows3(v_ref, at), table_ref[...], nhi, nlo)
        code = dir_ref[0:1, at]
        stays = code == 0
        rows = []
        for k in range(3):
            kept_ref[k : k + 1, at] = jnp.where(stays, new[k], 0.0)
            rows.extend(halves(new[k]))
            for j in range(per):
                seen[k, pl.ds(t * per + j, 1), :] = new[k][:, j * 128 : (j + 1) * 128]
        mask = one_hot(code - 1, 16)
        moved[...] += lax.dot_general(
            spread(rows, mask), one_hot(slot_ref[0:1, at], CAP), NT, preferred_element_type=F32
        )
        return carry

    def put(f, i, value):
        out_ref[f, i] = value

    sems = (out_sem, in_sem)
    rows_of_shift = [shift_ref.shape[0] - 1] * x_ref.shape[0]
    transfer = shift_fields(
        rows_of_shift, -1, shift_ref, x_ref, put, zbox, xbox, ybox, work, turned, faces, sems
    )
    particles = v_ref.shape[1]
    beside_work(transfer, step, particles // tile)
    for d in range(6):
        for k in range(3):
            going[d, k : k + 1, :] = (
                moved[32 * k + d : 32 * k + d + 1] + moved[32 * k + 16 + d : 32 * k + 17 + d]
            )
    copies = [
        send(going.at[d], coming.at[d], sems, 6 + d, AXES[d // 2], 1 - 2 * (d % 2)) for d in range(6)
    ]

    contacts = who_ref.shape[1]
    chunk = min(512, contacts)
    groups = seen.shape[1]
    sums = jnp.zeros((8 * 16, units), F32)
    parts = [halves(seen[k]) for k in range(3)]
    book = jnp.concatenate([jnp.concatenate(p, axis=1) for p in parts], axis=0)
    for c in range(contacts // chunk):
        at = slice(c * chunk, (c + 1) * chunk)
        hi, lo = split_index(who_ref[0:1, at], 128)
        hot = one_hot(lo, 128)
        got = jnp.dot(book, jnp.concatenate([hot, hot], axis=0), preferred_element_type=F32)
        here = lax.broadcasted_iota(jnp.int32, (groups, chunk), 0) == hi
        weight = weight_ref[0:1, at]
        rows = []
        for k in range(3):
            mine = jnp.where(here, got[k * groups : (k + 1) * groups], 0.0)
            rows.extend(halves(weight * jnp.sum(mine, axis=0, keepdims=True)))
        rows.extend(halves(weight))
        code, member = split_index(place_ref[0:1, at], units)
        sums = sums + lax.dot_general(
            spread(rows, one_hot(code, 16)), one_hot(member, units), NT, preferred_element_type=F32
        )
    totals = [sums[32 * k : 32 * k + 16] + sums[32 * k + 16 : 32 * k + 32] for k in range(4)]
    total = jnp.concatenate([t[6:7] for t in totals], axis=0)
    for d in range(6):
        for k in range(4):
            pushes[d, k : k + 1, :] = totals[k][d : d + 1]
    more = [
        send(pushes.at[d], pulls.at[d], sems, 12 + d, AXES[d // 2], 1 - 2 * (d % 2)) for d in range(6)
    ]
    for d, copy in enumerate(copies):
        copy.wait()
        kept_ref[:, particles + d * CAP : particles + (d + 1) * CAP] = coming[d, 0:3]
    for d, copy in enumerate(more):
        copy.wait()
        total = total + pulls[d]
    sum_w = total[3:4]
    force_ref[...] = (total[0:3] - sum_w * drift_ref[...]) / jnp.maximum(sum_w, 1.0)


AXES = ("gx", "gy", "gz")
MESH = pl.DeviceIdType.MESH


def beside(axis, sign):
    count = lax.axis_size(axis)
    return {axis: lax.rem(lax.axis_index(axis) + (sign + count), count)}


def greet():
    for axis in AXES:
        for sign in (1, -1):
            pl.semaphore_signal(
                pltpu.get_barrier_semaphore(), inc=1, device_id=beside(axis, sign), device_id_type=MESH
            )


def send(src, dst, sems, number, axis, sign):
    copy = pltpu.make_async_remote_copy(
        src_ref=src, dst_ref=dst, send_sem=sems[0].at[number], recv_sem=sems[1].at[number],
        device_id=beside(axis, sign), device_id_type=MESH,
    )
    copy.start()
    return copy


def both(pair, box, sems, number, axis):
    return [
        send(pair[0], box.at[0], sems, number, axis, -1),
        send(pair[1], box.at[1], sems, number + 1, axis, 1),
    ]


def shift_fields(rows, flip, shift_ref, x_ref, put, zbox, xbox, ybox, work, turned, faces, sems):
    n, cx, cy, nz = x_ref.shape
    ups = [[shift_ref[r, dim] * flip > 0 for dim in range(3)] for r in rows]
    greet()
    yield
    pl.semaphore_wait(pltpu.get_barrier_semaphore(), 6)
    copies = both((x_ref, x_ref), zbox, sems, 0, "gz")
    yield
    for copy in copies:
        copy.wait()
    for f in range(n):
        x = x_ref[f]
        plus = jnp.concatenate([x[:, :, 1:], zbox[0, f][:, :, 0:1]], axis=2)
        minus = jnp.concatenate([zbox[1, f][:, :, nz - 1 :], x[:, :, : nz - 1]], axis=2)
        work[f] = jnp.where(ups[f][2], plus, minus)
    copies = both((work.at[:, 0], work.at[:, cx - 1]), xbox, sems, 2, "gx")
    yield
    for copy in copies:
        copy.wait()
    for f in range(n):
        for i in range(cx):
            plus = work[f, i + 1] if i + 1 < cx else xbox[0, f]
            minus = work[f, i - 1] if i > 0 else xbox[1, f]
            row = jnp.where(ups[f][0], plus, minus)
            turned[f, i] = row
            faces[0, f, i : i + 1, :] = row[0:1]
            faces[1, f, i : i + 1, :] = row[cy - 1 :]
    copies = both((faces.at[0], faces.at[1]), ybox, sems, 4, "gy")
    yield
    for copy in copies:
        copy.wait()
    for f in range(n):
        for i in range(cx):
            x = turned[f, i]
            plus = jnp.concatenate([x[1:], ybox[0, f, i : i + 1, :]], axis=0)
            minus = jnp.concatenate([ybox[1, f, i : i + 1, :], x[: cy - 1]], axis=0)
            put(f, i, jnp.where(ups[f][1], plus, minus))


def shift_scratch(shape, kind):
    n, cx, cy, nz = shape
    return [
        pltpu.VMEM((2, n, cx, cy, nz), kind), pltpu.VMEM((2, n, cy, nz), kind),
        pltpu.VMEM((2, n, cx, nz), kind), pltpu.VMEM((n, cx, cy, nz), kind),
        pltpu.VMEM((n, cx, cy, nz), kind), pltpu.VMEM((2, n, cx, nz), kind),
    ]


def beside_work(transfer, step, tiles):
    for part in range(4):
        next(transfer)
        lax.fori_loop(tiles * part // 4, tiles * (part + 1) // 4, step, 0)
    for _ in transfer:
        pass


def contact_places(contact_colloid, units):
    size_x, size_y, size_z = (lax.axis_size(a) for a in ("gx", "gy", "gz"))
    mine_x, mine_y, mine_z = (lax.axis_index(a) for a in ("gx", "gy", "gz"))
    owner = contact_colloid // units
    apart_x = (owner // (size_y * size_z) - mine_x) % size_x
    apart_y = (owner // size_z % size_y - mine_y) % size_y
    apart_z = (owner % size_z - mine_z) % size_z
    code = jnp.full(owner.shape, 6, jnp.int32)
    for number, (apart, to) in reversed(
        list(
            enumerate(
                (
                    (apart_x, 1), (apart_x, size_x - 1), (apart_y, 1),
                    (apart_y, size_y - 1), (apart_z, 1), (apart_z, size_z - 1),
                )
            )
        )
    ):
        code = jnp.where(apart == to, number, code)
    return code * units + contact_colloid % units


def body(
    velocities, particle_cells, grid_shift, axis_index, migrate_dir, migrate_slot,
    contact_colloid, contact_particle, contact_weight, colloid_velocity,
):
    _, cx, cy, nlo = axis_index.shape
    nhi = cx * cy
    particles = velocities.shape[1]
    units = colloid_velocity.shape[1]
    tile = math.gcd(particles, TILE)
    mean_shape = jax.ShapeDtypeStruct((3, nhi, nlo), F32)
    acc = pltpu.VMEM((7 * nhi, nlo), F32)
    table = pltpu.VMEM((4 * nhi, 2 * nlo), BF)
    vmem = pl.BlockSpec(memory_space=pltpu.VMEM)
    smem = pl.BlockSpec(memory_space=pltpu.SMEM)

    def call(kernel, outs, scratch, number, *args):
        extra = {} if number is None else dict(collective_id=number, has_side_effects=True)
        first = vmem if number is None else smem
        return pl.pallas_call(
            functools.partial(kernel, tile, nhi, nlo),
            out_shape=outs,
            in_specs=[first] + [vmem] * (len(args) - 1),
            out_specs=tuple([vmem] * len(outs)),
            scratch_shapes=scratch,
            compiler_params=pltpu.CompilerParams(vmem_limit_bytes=48 * 2**20, **extra),
            cost_estimate=pl.CostEstimate(flops=10**9, bytes_accessed=30_000_000, transcendentals=0),
        )(*args)

    def semaphores(count):
        return [pltpu.SemaphoreType.DMA((count,)), pltpu.SemaphoreType.DMA((count,))]

    places = contact_places(contact_colloid, units)
    numbers = jax.ShapeDtypeStruct((nhi, nlo), jnp.int32)
    mean0, axis0, axis1 = call(
        first_kernel, (mean_shape, numbers, numbers),
        [acc] + shift_scratch(axis_index.shape, jnp.int32) + semaphores(6), 0,
        grid_shift, axis_index, particle_cells, velocities,
    )
    v1, mean1 = call(
        middle_kernel, (jax.ShapeDtypeStruct(velocities.shape, F32), mean_shape), [acc, table], None,
        particle_cells, velocities, mean0, axis0,
    )
    grid_mean = mean1.reshape(3, cx, cy, nlo)
    return call(
        lambda t, h, l, *refs: last_kernel(t, h, l, units, *refs),
        (
            jax.ShapeDtypeStruct(grid_mean.shape, F32),
            jax.ShapeDtypeStruct((3, particles + 6 * CAP), F32),
            jax.ShapeDtypeStruct((3, units), F32),
        ),
        [pltpu.VMEM((96, CAP), F32), table, pltpu.VMEM((3, particles // 128, 128), F32)]
        + [pltpu.VMEM((6, 3, CAP), F32)] * 2
        + [pltpu.VMEM((6, 4, units), F32)] * 2
        + shift_scratch(grid_mean.shape, F32)
        + semaphores(18),
        1,
        grid_shift, grid_mean, particle_cells, v1, mean1, axis1, migrate_dir.reshape(1, -1),
        migrate_slot.reshape(1, -1), places.reshape(1, -1), contact_particle.reshape(1, -1),
        contact_weight.reshape(1, -1), colloid_velocity,
    )


def solution(mesh):
    flat = P(None, ("gx", "gy", "gz"))
    line = P(("gx", "gy", "gz"))
    grid = P(None, "gx", "gy", "gz")
    return jax.shard_map(
        body,
        mesh=mesh,
        in_specs=(flat, flat, P(), grid, line, line, line, line, line, flat),
        out_specs=(grid, flat, flat),
        check_vma=False,
    )
```

```python
import functools
import math

import jax
import jax.numpy as jnp
from jax import lax
from jax.experimental import pallas as pl
from jax.experimental.pallas import tpu as pltpu
from jax.sharding import PartitionSpec as P

CAP = 160
ANGLE = 130.0 * math.pi / 180.0
COS, SIN = math.cos(ANGLE), math.sin(ANGLE)
TILE = 4096
NT = (((1,), (1,)), ((), ()))
BF = jnp.bfloat16
F32 = jnp.float32


def split_index(c, low):
    if low & (low - 1) == 0:
        return c >> (low.bit_length() - 1), c & (low - 1)
    return c // low, c % low


def one_hot(row, count):
    kind = BF if count <= 256 else F32
    wide = lax.broadcasted_iota(jnp.int32, (count, row.shape[1]), 0).astype(F32).astype(kind)
    return jnp.where(wide == row.astype(F32).astype(kind), jnp.ones((), kind), jnp.zeros((), kind)).astype(BF)


def halves(x):
    high = x.astype(BF)
    return high, (x - high.astype(F32)).astype(BF)


def spread(rows, mask):
    return jnp.concatenate([mask * row for row in rows], axis=0)


def hist_tile(c, v, nhi, nlo):
    hi, lo = split_index(c, nlo)
    mask = one_hot(hi, nhi)
    rows = []
    for k in range(3):
        rows.extend(halves(v[k]))
    left = jnp.concatenate([spread(rows, mask), mask], axis=0)
    return lax.dot_general(left, one_hot(lo, nlo), NT, preferred_element_type=F32)


def mean_of(acc, mean_ref, nhi):
    count = jnp.maximum(acc[6 * nhi : 7 * nhi], 1.0)
    for k in range(3):
        total = acc[2 * k * nhi : (2 * k + 1) * nhi] + acc[(2 * k + 1) * nhi : (2 * k + 2) * nhi]
        mean_ref[k] = total / count


def signs_of(index):
    return [jnp.where((index & (1 << i)) != 0, 1.0, -1.0) for i in range(3)]


def rotate(e, v):
    along = ((1.0 - COS) / 3.0) * (e[0] * v[0] + e[1] * v[1] + e[2] * v[2])
    turn = SIN / math.sqrt(3.0)
    out = []
    for i in range(3):
        j, k = (i + 1) % 3, (i + 2) % 3
        out.append(COS * v[i] + e[i] * along + turn * (e[j] * v[k] - e[k] * v[j]))
    return out


def make_table(mean_ref, axis_ref, table_ref, nhi, nlo):
    mean = [mean_ref[k] for k in range(3)]
    index = axis_ref[...]
    turned = rotate(signs_of(index), mean)
    for k in range(3):
        high, low = halves(mean[k] - turned[k])
        table_ref[k * nhi : (k + 1) * nhi, 0:nlo] = high
        table_ref[k * nhi : (k + 1) * nhi, nlo : 2 * nlo] = low
    table_ref[3 * nhi : 4 * nhi, 0:nlo] = index.astype(F32).astype(BF)
    table_ref[3 * nhi : 4 * nhi, nlo : 2 * nlo] = jnp.zeros((nhi, nlo), BF)


def collide_tile(c, v, table, nhi, nlo):
    hi, lo = split_index(c, nlo)
    hot = one_hot(lo, nlo)
    got = jnp.dot(table, jnp.concatenate([hot, hot], axis=0), preferred_element_type=F32)
    here = lax.broadcasted_iota(jnp.int32, (nhi, c.shape[1]), 0) == hi
    picked = [
        jnp.sum(jnp.where(here, got[q * nhi : (q + 1) * nhi], 0.0), axis=0, keepdims=True)
        for q in range(4)
    ]
    turned = rotate(signs_of(picked[3].astype(jnp.int32)), v)
    return [turned[k] + picked[k] for k in range(3)]


def rows3(ref, at):
    return [ref[k : k + 1, at] for k in range(3)]


def first_kernel(
    tile, nhi, nlo, shift_ref, x_ref, cell_ref, v_ref, mean_ref, axis0_ref, axis1_ref,
    acc, zbox, xbox, ybox, work, turned, faces, out_sem, in_sem
):
    acc[...] = jnp.zeros_like(acc)
    cy = x_ref.shape[2]

    def put(f, i, value):
        (axis0_ref, axis1_ref)[f][i * cy : (i + 1) * cy, :] = value

    def step(t, carry):
        at = pl.ds(pl.multiple_of(t * tile, tile), tile)
        acc[...] += hist_tile(cell_ref[0:1, at], rows3(v_ref, at), nhi, nlo)
        return carry

    transfer = shift_fields(
        (0, 1), 1, shift_ref, x_ref, put, zbox, xbox, ybox, work, turned, faces, (out_sem, in_sem)
    )
    beside_work(transfer, step, v_ref.shape[1] // tile)
    mean_of(acc, mean_ref, nhi)


def middle_kernel(
    tile, nhi, nlo, cell_ref, v_ref, mean_ref, axis_ref, next_ref, next_mean_ref, acc, table_ref
):
    acc[...] = jnp.zeros_like(acc)
    make_table(mean_ref, axis_ref, table_ref, nhi, nlo)

    def step(t, carry):
        at = pl.ds(pl.multiple_of(t * tile, tile), tile)
        new = collide_tile(cell_ref[0:1, at], rows3(v_ref, at), table_ref[...], nhi, nlo)
        for k in range(3):
            next_ref[k : k + 1, at] = new[k]
        acc[...] += hist_tile(cell_ref[1:2, at], new, nhi, nlo)
        return carry

    lax.fori_loop(0, v_ref.shape[1] // tile, step, 0)
    mean_of(acc, next_mean_ref, nhi)


def last_kernel(
    tile, nhi, nlo, units, shift_ref, x_ref, cell_ref, v_ref, mean_ref, axis_ref, dir_ref, slot_ref,
    place_ref, who_ref, weight_ref, drift_ref, out_ref, kept_ref, force_ref, moved, table_ref, seen,
    going, coming, pushes, pulls, zbox, xbox, ybox, work, turned, faces, out_sem, in_sem
):
    moved[...] = jnp.zeros_like(moved)
    make_table(mean_ref, axis_ref, table_ref, nhi, nlo)
    per = tile // 128

    def step(t, carry):
        at = pl.ds(pl.multiple_of(t * tile, tile), tile)
        new = collide_tile(cell_ref[1:2, at], rows3(v_ref, at), table_ref[...], nhi, nlo)
        code = dir_ref[0:1, at]
        stays = code == 0
        rows = []
        for k in range(3):
            kept_ref[k : k + 1, at] = jnp.where(stays, new[k], 0.0)
            rows.extend(halves(new[k]))
            for j in range(per):
                seen[k, pl.ds(t * per + j, 1), :] = new[k][:, j * 128 : (j + 1) * 128]
        mask = one_hot(code - 1, 16)
        moved[...] += lax.dot_general(
            spread(rows, mask), one_hot(slot_ref[0:1, at], CAP), NT, preferred_element_type=F32
        )
        return carry

    def put(f, i, value):
        out_ref[f, i] = value

    sems = (out_sem, in_sem)
    rows_of_shift = [shift_ref.shape[0] - 1] * x_ref.shape[0]
    transfer = shift_fields(
        rows_of_shift, -1, shift_ref, x_ref, put, zbox, xbox, ybox, work, turned, faces, sems
    )
    particles = v_ref.shape[1]
    beside_work(transfer, step, particles // tile)
    for d in range(6):
        for k in range(3):
            going[d, k : k + 1, :] = (
                moved[32 * k + d : 32 * k + d + 1] + moved[32 * k + 16 + d : 32 * k + 17 + d]
            )
    copies = [
        send(going.at[d], coming.at[d], sems, 6 + d, AXES[d // 2], 1 - 2 * (d % 2)) for d in range(6)
    ]

    contacts = who_ref.shape[1]
    chunk = min(512, contacts)
    groups = seen.shape[1]
    sums = jnp.zeros((8 * 16, units), F32)
    parts = [halves(seen[k]) for k in range(3)]
    book = jnp.concatenate([jnp.concatenate(p, axis=1) for p in parts], axis=0)
    for c in range(contacts // chunk):
        at = slice(c * chunk, (c + 1) * chunk)
        hi, lo = split_index(who_ref[0:1, at], 128)
        hot = one_hot(lo, 128)
        got = jnp.dot(book, jnp.concatenate([hot, hot], axis=0), preferred_element_type=F32)
        here = lax.broadcasted_iota(jnp.int32, (groups, chunk), 0) == hi
        weight = weight_ref[0:1, at]
        rows = []
        for k in range(3):
            mine = jnp.where(here, got[k * groups : (k + 1) * groups], 0.0)
            rows.extend(halves(weight * jnp.sum(mine, axis=0, keepdims=True)))
        rows.extend(halves(weight))
        code, member = split_index(place_ref[0:1, at], units)
        sums = sums + lax.dot_general(
            spread(rows, one_hot(code, 16)), one_hot(member, units), NT, preferred_element_type=F32
        )
    totals = [sums[32 * k : 32 * k + 16] + sums[32 * k + 16 : 32 * k + 32] for k in range(4)]
    total = jnp.concatenate([t[6:7] for t in totals], axis=0)
    for d in range(6):
        for k in range(4):
            pushes[d, k : k + 1, :] = totals[k][d : d + 1]
    more = [
        send(pushes.at[d], pulls.at[d], sems, 12 + d, AXES[d // 2], 1 - 2 * (d % 2)) for d in range(6)
    ]
    for d, copy in enumerate(copies):
        copy.wait()
        kept_ref[:, particles + d * CAP : particles + (d + 1) * CAP] = coming[d, 0:3]
    for d, copy in enumerate(more):
        copy.wait()
        total = total + pulls[d]
    sum_w = total[3:4]
    force_ref[...] = (total[0:3] - sum_w * drift_ref[...]) / jnp.maximum(sum_w, 1.0)


AXES = ("gx", "gy", "gz")
MESH = pl.DeviceIdType.MESH


def beside(axis, sign):
    count = lax.axis_size(axis)
    return {axis: lax.rem(lax.axis_index(axis) + (sign + count), count)}


def greet():
    for axis in AXES:
        for sign in (1, -1):
            pl.semaphore_signal(
                pltpu.get_barrier_semaphore(), inc=1, device_id=beside(axis, sign), device_id_type=MESH
            )


def send(src, dst, sems, number, axis, sign):
    copy = pltpu.make_async_remote_copy(
        src_ref=src, dst_ref=dst, send_sem=sems[0].at[number], recv_sem=sems[1].at[number],
        device_id=beside(axis, sign), device_id_type=MESH,
    )
    copy.start()
    return copy


def both(pair, box, sems, number, axis):
    return [
        send(pair[0], box.at[0], sems, number, axis, -1),
        send(pair[1], box.at[1], sems, number + 1, axis, 1),
    ]


def shift_fields(rows, flip, shift_ref, x_ref, put, zbox, xbox, ybox, work, turned, faces, sems):
    n, cx, cy, nz = x_ref.shape
    ups = [[shift_ref[r, dim] * flip > 0 for dim in range(3)] for r in rows]
    greet()
    yield
    pl.semaphore_wait(pltpu.get_barrier_semaphore(), 6)
    copies = both((x_ref, x_ref), zbox, sems, 0, "gz")
    yield
    for copy in copies:
        copy.wait()
    for f in range(n):
        x = x_ref[f]
        plus = jnp.concatenate([x[:, :, 1:], zbox[0, f][:, :, 0:1]], axis=2)
        minus = jnp.concatenate([zbox[1, f][:, :, nz - 1 :], x[:, :, : nz - 1]], axis=2)
        work[f] = jnp.where(ups[f][2], plus, minus)
    copies = both((work.at[:, 0], work.at[:, cx - 1]), xbox, sems, 2, "gx")
    yield
    for copy in copies:
        copy.wait()
    for f in range(n):
        for i in range(cx):
            plus = work[f, i + 1] if i + 1 < cx else xbox[0, f]
            minus = work[f, i - 1] if i > 0 else xbox[1, f]
            row = jnp.where(ups[f][0], plus, minus)
            turned[f, i] = row
            faces[0, f, i : i + 1, :] = row[0:1]
            faces[1, f, i : i + 1, :] = row[cy - 1 :]
    copies = both((faces.at[0], faces.at[1]), ybox, sems, 4, "gy")
    yield
    for copy in copies:
        copy.wait()
    for f in range(n):
        for i in range(cx):
            x = turned[f, i]
            plus = jnp.concatenate([x[1:], ybox[0, f, i : i + 1, :]], axis=0)
            minus = jnp.concatenate([ybox[1, f, i : i + 1, :], x[: cy - 1]], axis=0)
            put(f, i, jnp.where(ups[f][1], plus, minus))


def shift_scratch(shape, kind):
    n, cx, cy, nz = shape
    return [
        pltpu.VMEM((2, n, cx, cy, nz), kind), pltpu.VMEM((2, n, cy, nz), kind),
        pltpu.VMEM((2, n, cx, nz), kind), pltpu.VMEM((n, cx, cy, nz), kind),
        pltpu.VMEM((n, cx, cy, nz), kind), pltpu.VMEM((2, n, cx, nz), kind),
    ]


def beside_work(transfer, step, tiles):
    for part in range(4):
        next(transfer)
        lax.fori_loop(tiles * part // 4, tiles * (part + 1) // 4, step, 0)
    for _ in transfer:
        pass


def contact_places(contact_colloid, units):
    size_x, size_y, size_z = (lax.axis_size(a) for a in ("gx", "gy", "gz"))
    mine_x, mine_y, mine_z = (lax.axis_index(a) for a in ("gx", "gy", "gz"))
    owner = contact_colloid // units
    apart_x = (owner // (size_y * size_z) - mine_x) % size_x
    apart_y = (owner // size_z % size_y - mine_y) % size_y
    apart_z = (owner % size_z - mine_z) % size_z
    code = jnp.full(owner.shape, 6, jnp.int32)
    for number, (apart, to) in reversed(
        list(
            enumerate(
                (
                    (apart_x, 1), (apart_x, size_x - 1), (apart_y, 1),
                    (apart_y, size_y - 1), (apart_z, 1), (apart_z, size_z - 1),
                )
            )
        )
    ):
        code = jnp.where(apart == to, number, code)
    return code * units + contact_colloid % units


def body(
    velocities, particle_cells, grid_shift, axis_index, migrate_dir, migrate_slot,
    contact_colloid, contact_particle, contact_weight, colloid_velocity,
):
    _, cx, cy, nlo = axis_index.shape
    nhi = cx * cy
    particles = velocities.shape[1]
    units = colloid_velocity.shape[1]
    tile = math.gcd(particles, TILE)
    mean_shape = jax.ShapeDtypeStruct((3, nhi, nlo), F32)
    acc = pltpu.VMEM((7 * nhi, nlo), F32)
    table = pltpu.VMEM((4 * nhi, 2 * nlo), BF)
    vmem = pl.BlockSpec(memory_space=pltpu.VMEM)
    smem = pl.BlockSpec(memory_space=pltpu.SMEM)

    def call(kernel, outs, scratch, number, *args):
        extra = {} if number is None else dict(collective_id=number, has_side_effects=True)
        first = vmem if number is None else smem
        return pl.pallas_call(
            functools.partial(kernel, tile, nhi, nlo),
            out_shape=outs,
            in_specs=[first] + [vmem] * (len(args) - 1),
            out_specs=tuple([vmem] * len(outs)),
            scratch_shapes=scratch,
            compiler_params=pltpu.CompilerParams(vmem_limit_bytes=48 * 2**20, **extra),
            cost_estimate=pl.CostEstimate(flops=10**9, bytes_accessed=30_000_000, transcendentals=0),
        )(*args)

    def semaphores(count):
        return [pltpu.SemaphoreType.DMA((count,)), pltpu.SemaphoreType.DMA((count,))]

    places = contact_places(contact_colloid, units)
    numbers = jax.ShapeDtypeStruct((nhi, nlo), jnp.int32)
    mean0, axis0, axis1 = call(
        first_kernel, (mean_shape, numbers, numbers),
        [acc] + shift_scratch(axis_index.shape, jnp.int32) + semaphores(6), 0,
        grid_shift, axis_index, particle_cells, velocities,
    )
    v1, mean1 = call(
        middle_kernel, (jax.ShapeDtypeStruct(velocities.shape, F32), mean_shape), [acc, table], None,
        particle_cells, velocities, mean0, axis0,
    )
    grid_mean = mean1.reshape(3, cx, cy, nlo)
    return call(
        lambda t, h, l, *refs: last_kernel(t, h, l, units, *refs),
        (
            jax.ShapeDtypeStruct(grid_mean.shape, F32),
            jax.ShapeDtypeStruct((3, particles + 6 * CAP), F32),
            jax.ShapeDtypeStruct((3, units), F32),
        ),
        [pltpu.VMEM((96, CAP), F32), table, pltpu.VMEM((3, particles // 128, 128), F32)]
        + [pltpu.VMEM((6, 3, CAP), F32)] * 2
        + [pltpu.VMEM((6, 4, units), F32)] * 2
        + shift_scratch(grid_mean.shape, F32)
        + semaphores(18),
        1,
        grid_shift, grid_mean, particle_cells, v1, mean1, axis1, migrate_dir.reshape(1, -1),
        migrate_slot.reshape(1, -1), places.reshape(1, -1), contact_particle.reshape(1, -1),
        contact_weight.reshape(1, -1), colloid_velocity,
    )


def solution(mesh):
    flat = P(None, ("gx", "gy", "gz"))
    line = P(("gx", "gy", "gz"))
    grid = P(None, "gx", "gy", "gz")
    return jax.shard_map(
        body,
        mesh=mesh,
        in_specs=(flat, flat, P(), grid, line, line, line, line, line, flat),
        out_specs=(grid, flat, flat),
        check_vma=False,
    )
```
